512 devices in a mesh: ctx: 64 (over y, z), tp: 8 (over x, core).
Axes of the slice: x: 4, y: 8, z: 8, core: 2. Of those that a mesh axis runs over, the one named last changes fastest.
Arguments:
- x_heads: bfloat16 [16384, 5120], P('ctx', 'tp'), may hold values from -6 to 6
- log_decay: float32 [80, 16384], P('tp', 'ctx'), may hold values from -1 to 0, as said below
- b_proj: bfloat16 [16384, 128], P('ctx'), may hold values from -6 to 6
- c_proj: bfloat16 [16384, 128], P('ctx'), may hold values from -6 to 6
- grad_out: bfloat16 [16384, 5120], P('ctx', 'tp'), may hold values from -0.00390625 to 0.00390625
Outputs:
- grad_x: bfloat16 [16384, 5120], P('ctx', 'tp')
- grad_b: float32 [16384, 128], P(('ctx', 'tp'))
- grad_c: float32 [16384, 128], P(('ctx', 'tp'))
The draws below stay inside these ranges and needn't reach their ends.
Inputs may be any that keep to these rules, and one draw needn't show every extreme that they name: log_decay is negative everywhere.
All inputs are finite; a program needn't handle non-finite values.
Results may differ from the reference program's by a relative error of at most 0.0056.
Values sent between devices are 32-bit elements; how exact they have to be, the bound alone decides.
A program may use at most 128 MiB of HBM per device.

```python
import jax
import jax.numpy as jnp
from jax import lax

HEADS = 80
HEADDIM = 64
STATE = 128
GROUP = 256
SEQ = 16384


def draw_log_decay(key, part):
    keys = jax.random.split(key, 6)
    slow_share = 0.5
    slow = jax.random.uniform(keys[0], (HEADS, 1)) < slow_share
    slow_rate = jnp.exp(jax.random.uniform(keys[1], (HEADS, 1), minval=jnp.log(0.08), maxval=jnp.log(0.8))) / SEQ
    fast_rate = jnp.exp(jax.random.uniform(keys[2], (HEADS, 1), minval=jnp.log(1.0 / 50.0), maxval=jnp.log(1.0 / 30.0)))
    decay_speed = jnp.where(slow, slow_rate, fast_rate)
    coarse_estimate = jnp.exp(jax.random.uniform(keys[3], (HEADS, SEQ), minval=jnp.log(0.5), maxval=jnp.log(2.0)))
    places = jax.random.randint(keys[4], (HEADS, 2), 0, SEQ)
    match_count = jnp.arange(SEQ)[None, None, :] == places[:, :, None]
    decay_falls = jnp.log(jax.random.uniform(keys[5], (HEADS, 2, 1), minval=0.5, maxval=0.8))
    spike_amount = jnp.sum(jnp.where(match_count, decay_falls, 0.0), axis=1)
    return (-decay_speed * coarse_estimate + spike_amount).astype(jnp.float32)


def levels(stream_key, dims, cuts, smallest, top_value):
    gain, own = 1.0, jax.random.fold_in(stream_key, 6)
    for axis_at, parts in cuts:
        heights = jnp.exp(jax.random.uniform(jax.random.fold_in(own, axis_at), (parts,), jnp.float32, smallest / len(cuts), top_value / len(cuts)))
        gain = gain * jnp.repeat(heights, dims[axis_at] // parts).reshape([-1 if axis == axis_at else 1 for axis in range(len(dims))])
    return gain


def centred(key, dims, scale, bound, cuts=(), held_as=jnp.bfloat16):
    values = scale * jax.random.normal(key, dims, jnp.float32)
    if cuts:
        values = values * levels(key, dims, cuts, -0.22, 0.18)
    return jnp.clip(values, -bound, bound).astype(held_as)


def setup_inputs(seed: int = 0) -> dict:
    arg_keys = jax.random.split(jax.random.key(seed), 6)
    x_heads = centred(arg_keys[0], (SEQ, HEADS * HEADDIM), 1.0, 6.0, ((0, 64), (1, 8)))
    log_decay = draw_log_decay(jax.random.fold_in(arg_keys[5], 71), 0)
    b_proj = centred(arg_keys[2], (SEQ, STATE), 0.8, 6.0, ((0, 64),))
    c_proj = centred(arg_keys[3], (SEQ, STATE), 0.8, 6.0, ((0, 64),))
    grad_out = centred(arg_keys[4], (SEQ, HEADS * HEADDIM), (STATE * SEQ) ** -0.5, 0.00390625, ((0, 64), (1, 8)))
    return dict(x_heads=x_heads, log_decay=log_decay, b_proj=b_proj, c_proj=c_proj, grad_out=grad_out)


def reference(x_heads, log_decay, b_proj, c_proj, grad_out):
    nblock = SEQ // GROUP
    xs = x_heads.reshape(nblock, GROUP, HEADS, HEADDIM)
    gs = grad_out.reshape(nblock, GROUP, HEADS, HEADDIM)
    bs = b_proj.reshape(nblock, GROUP, STATE)
    cs = c_proj.reshape(nblock, GROUP, STATE)
    cums = jnp.cumsum(log_decay.reshape(HEADS, nblock, GROUP), axis=2).transpose(1, 0, 2)
    lower = jnp.arange(GROUP)[:, None] >= jnp.arange(GROUP)[None, :]

    def forward(state, inputs):
        xk, bk, cumk = inputs
        last = cumk[:, -1]
        weight = jnp.exp(last[:, None] - cumk)
        xw = (xk.astype(jnp.float32) * weight.T[:, :, None]).astype(jnp.bfloat16)
        xw = lax.optimization_barrier(xw).astype(jnp.float32)
        summ = jnp.einsum('qn,qhp->hnp', bk.astype(jnp.float32), xw)
        return jnp.exp(last)[:, None, None] * state + summ, state.astype(jnp.bfloat16)

    zero = jnp.zeros((HEADS, STATE, HEADDIM), jnp.float32)
    _, incoming_state = lax.scan(forward, zero, (xs, bs, cums))

    def backward(carry, inputs):
        xk, gk, bk, ck, cumk, hk = inputs
        last = cumk[:, -1]
        decay = jnp.where(lower[None], jnp.exp(jnp.minimum(cumk[:, :, None] - cumk[:, None, :], 0.0)), 0.0)
        xf = xk.astype(jnp.float32)
        gf = gk.astype(jnp.float32)
        bf = bk.astype(jnp.float32)
        cf = ck.astype(jnp.float32)
        mixed = jnp.einsum('qhp,shp->hqs', gf, xf)
        first = lax.optimization_barrier((mixed * decay).astype(jnp.bfloat16)).astype(jnp.float32)
        gram = jnp.dot(ck, bk.T, preferred_element_type=jnp.float32)
        third = lax.optimization_barrier((gram[None] * decay).astype(jnp.bfloat16)).astype(jnp.float32)
        after = lax.optimization_barrier(carry.astype(jnp.bfloat16)).astype(jnp.float32)
        hin = hk.astype(jnp.float32)
        head_w = jnp.exp(cumk)
        tail = jnp.exp(last[:, None] - cumk)
        grad_c = jnp.einsum('hqs,sn->qn', first, bf) + jnp.sum(head_w[:, :, None] * jnp.einsum('qhp,hnp->hqn', gf, hin), axis=0)
        grad_b = jnp.einsum('hsq,sn->qn', first, cf) + jnp.sum(tail[:, :, None] * jnp.einsum('qhp,hnp->hqn', xf, after), axis=0)
        grad_x = jnp.einsum('hsq,shp->qhp', third, gf) + tail.T[:, :, None] * jnp.einsum('qn,hnp->qhp', bf, after)
        gw = (gf * head_w.T[:, :, None]).astype(jnp.bfloat16)
        gw = lax.optimization_barrier(gw).astype(jnp.float32)
        upd = jnp.einsum('qn,qhp->hnp', cf, gw)
        return upd + jnp.exp(last)[:, None, None] * carry, (grad_x.astype(jnp.bfloat16), grad_b, grad_c)

    _, (grad_x, grad_b, grad_c) = lax.scan(backward, zero, (xs, gs, bs, cs, cums, incoming_state), reverse=True)
    return (grad_x.reshape(SEQ, HEADS * HEADDIM), grad_b.reshape(SEQ, STATE).astype(jnp.float32), grad_c.reshape(SEQ, STATE).astype(jnp.float32))
```

```python
import functools

import jax
import jax.numpy as jnp
from jax import lax
from jax.experimental import pallas as pl
from jax.experimental.pallas import tpu as pltpu
from jax.sharding import PartitionSpec as P

HEADDIM = 64
STATE = 128
GROUP = 256
HALVES = 2
FORWARD, BACKWARD = 0, 1
MESH = pl.DeviceIdType.MESH
F32, BF16 = jnp.float32, jnp.bfloat16
NT = (((1,), (1,)), ((), ()))


def grid_of(blocks):
    rows = 1
    while rows * rows < blocks:
        rows *= 2
    return blocks // rows, rows


def ring_offset(step, size):
    return size // 2 + ((step + 1) // 2) * (2 * (step % 2) - 1)


def kernel(
    ny, nz, nt,
    x_hbm, ld_hbm, b_hbm, c_hbm, g_hbm,
    gx_hbm, gb_out, gc_out,
    x_v, ld_v, b_v, c_v, g_v, xw_v, gw_v, tail_v, cols_v, row_v,
    own_dec, dec_z, dec_y, own_row, edge,
    states, rec_z, pre, total, rec_y, back, ret, hbf,
    acc_f, gx_acc, gx_bf, part, rec_t,
    load_sem, out_sem,
    dz_send, dz_recv, dy_send, dy_recv, z_send, z_recv, y_send, y_recv, r_send, r_recv, t_send, t_recv,
):
    heads = ld_v.shape[0]
    width = x_v.shape[1]
    pairs = width // 128
    piece = STATE // nz
    half = piece // HALVES
    rows = GROUP // nt
    me = lax.axis_index("ctx")
    me_t = lax.axis_index("tp")
    me_y, me_z = me // nz, lax.rem(me, nz)

    def at_z(z):
        return {"ctx": me_y * nz + z}

    def at_y(y):
        return {"ctx": y * nz + me_z}

    def at_t(t):
        return {"tp": t}

    loads = [
        pltpu.make_async_copy(src, dst, load_sem.at[i])
        for i, (src, dst) in enumerate(
            ((ld_hbm, ld_v), (b_hbm, b_v), (x_hbm, x_v), (c_hbm, c_v), (g_hbm, g_v))
        )
    ]
    for load in loads:
        load.start()

    barrier = pltpu.get_barrier_semaphore()

    def greet(to, size, mine):
        def body(i, carry):
            pl.semaphore_signal(
                barrier, inc=1, device_id=to(lax.rem(mine + 1 + i, size)), device_id_type=MESH
            )
            return carry

        lax.fori_loop(0, size - 1, body, 0)

    greet(at_z, nz, me_z)
    greet(at_y, ny, me_y)
    greet(at_t, nt, me_t)

    loads[0].wait()
    ld = ld_v[...]
    at_r = lax.broadcasted_iota(jnp.int32, (GROUP, GROUP), 0)
    at_c = lax.broadcasted_iota(jnp.int32, (GROUP, GROUP), 1)
    upper = (at_r <= at_c).astype(F32)
    lower = (at_r >= at_c).astype(F32)
    high = lax.Precision.HIGHEST
    row_v[...] = jnp.dot(ld, upper, precision=high, preferred_element_type=F32)
    cum_t = lax.dot_general(lower, ld, NT, precision=high, preferred_element_type=F32)
    lane = lax.broadcasted_iota(jnp.int32, (GROUP, 128), 1)
    left = lane < HEADDIM
    for h in range(heads):
        cols_v[h] = jnp.broadcast_to(cum_t[:, h : h + 1], (GROUP, 128))

    loads[1].wait()
    loads[2].wait()
    for p in range(pairs):
        at = slice(p * 128, p * 128 + 128)
        cum = jnp.where(left, cols_v[2 * p], cols_v[2 * p + 1])
        last = cum[GROUP - 1 : GROUP, :]
        tail = jnp.exp(last - cum)
        tail_v[:, at] = tail
        xw_v[:, at] = (x_v[:, at].astype(F32) * tail).astype(BF16)
        own_dec[:, at] = jnp.exp(last)
    bt = b_v[...].astype(F32).T.astype(BF16)
    states[FORWARD] = jnp.dot(bt, xw_v[...], preferred_element_type=F32)

    pl.semaphore_wait(barrier, nz + ny + nt - 3)

    def over(size, fn):
        def body(i, carry):
            fn(i)
            return carry

        lax.fori_loop(0, size, body, 0)

    def dec_z_copy(i):
        to = lax.rem(me_z + ring_offset(i, nz), nz)
        return pltpu.make_async_remote_copy(
            own_dec, dec_z.at[me_z], dz_send.at[to], dz_recv.at[me_z], at_z(to), MESH
        )

    def z_copy(way, part_at, i):
        to = lax.rem(me_z + ring_offset(i, nz), nz)
        chunk = way * HALVES + part_at
        return pltpu.make_async_remote_copy(
            states.at[way, pl.ds(pl.multiple_of(to * piece + part_at * half, half), half)],
            rec_z.at[way, part_at, me_z],
            z_send.at[chunk, to],
            z_recv.at[chunk, me_z],
            at_z(to),
            MESH,
        )

    def keep_own(way):
        for part_at in range(HALVES):
            rec_z[way, part_at, me_z] = states[
                way, pl.ds(pl.multiple_of(me_z * piece + part_at * half, half), half)
            ]

    over(nz - 1, lambda i: dec_z_copy(i).start())
    for part_at in range(HALVES):
        over(nz - 1, lambda i: z_copy(FORWARD, part_at, i).start())
    dec_z[me_z] = own_dec[...]
    keep_own(FORWARD)

    loads[3].wait()
    loads[4].wait()
    for p in range(pairs):
        at = slice(p * 128, p * 128 + 128)
        cum = jnp.where(left, cols_v[2 * p], cols_v[2 * p + 1])
        gw_v[:, at] = (g_v[:, at].astype(F32) * jnp.exp(cum)).astype(BF16)
    ct = c_v[...].astype(F32).T.astype(BF16)
    states[BACKWARD] = jnp.dot(ct, gw_v[...], preferred_element_type=F32)
    for part_at in range(HALVES):
        over(nz - 1, lambda i: z_copy(BACKWARD, part_at, i).start())
    keep_own(BACKWARD)

    gram_t = lax.dot_general(b_v[...], c_v[...], NT, preferred_element_type=F32)
    hb = GROUP // 2
    tri = (
        lax.broadcasted_iota(jnp.int32, (hb, hb), 0) <= lax.broadcasted_iota(jnp.int32, (hb, hb), 1)
    )
    lane_b = lax.broadcasted_iota(jnp.int32, (1, 128), 1)
    sides = ((lane_b < HEADDIM).astype(BF16), (lane_b >= HEADDIM).astype(BF16))
    tiles = ((0, 0), (0, 1), (1, 1))
    for p in range(pairs):
        at = slice(p * 128, p * 128 + 128)
        xp, gp = x_v[:, at], g_v[:, at]
        out = [jnp.zeros((hb, 128), F32) for _ in range(2)]
        for side in range(2):
            h = 2 * p + side
            gm = gp * sides[side]
            for ib, ub in tiles:
                mi, mu = slice(ib * hb, ib * hb + hb), slice(ub * hb, ub * hb + hb)
                mixed_t = lax.dot_general(xp[mi], gm[mu], NT, preferred_element_type=F32)
                decay_t = jnp.exp(jnp.minimum(row_v[h : h + 1, mu] - cols_v[h, mi, :], 0.0))
                if ib == ub:
                    decay_t = jnp.where(tri, decay_t, 0.0)
                first_t = mixed_t * decay_t
                if h == 0:
                    acc_f[mi, mu] = first_t
                else:
                    acc_f[mi, mu] += first_t
                third_t = (gram_t[mi, mu] * decay_t).astype(BF16)
                out[ib] = out[ib] + jnp.dot(third_t, gm[mu], preferred_element_type=F32)
        gx_acc[:hb, at] = out[0]
        gx_acc[hb:, at] = out[1]
    acc_f[hb:, :hb] = jnp.zeros((hb, hb), F32)
    first_t = acc_f[...]
    part[1] = jnp.dot(first_t.astype(BF16), c_v[...], preferred_element_type=F32)
    part[0] = jnp.dot(first_t.T.astype(BF16), b_v[...], preferred_element_type=F32)

    def wait_dec(i):
        src = lax.rem(me_z + ring_offset(i, nz), nz)
        pltpu.make_async_remote_copy(
            own_dec, dec_z.at[src], dz_send.at[src], dz_recv.at[src], at_z(src), MESH
        ).wait_recv()

    over(nz - 1, wait_dec)
    ahead = jnp.ones((1, width), F32)
    for z in range(nz):
        edge[FORWARD, z] = ahead
        ahead = ahead * dec_z[z]
    own_row[...] = ahead
    behind = jnp.ones((1, width), F32)
    for z in reversed(range(nz)):
        edge[BACKWARD, z] = behind
        behind = behind * dec_z[z]

    def dec_y_copy(i):
        to = lax.rem(me_y + ring_offset(i, ny), ny)
        return pltpu.make_async_remote_copy(
            own_row, dec_y.at[me_y], dy_send.at[to], dy_recv.at[me_y], at_y(to), MESH
        )

    over(ny - 1, lambda i: dec_y_copy(i).start())

    def y_copy(way, part_at, y):
        chunk = way * HALVES + part_at
        return pltpu.make_async_remote_copy(
            total.at[way, part_at],
            rec_y.at[way, part_at, me_y],
            y_send.at[chunk, y],
            y_recv.at[chunk, me_y],
            at_y(y),
            MESH,
        )

    def y_from(way, part_at, y):
        chunk = way * HALVES + part_at
        return pltpu.make_async_remote_copy(
            total.at[way, part_at],
            rec_y.at[way, part_at, y],
            y_send.at[chunk, y],
            y_recv.at[chunk, y],
            at_y(y),
            MESH,
        )

    def y_targets(way, fn):
        def body(y, carry):
            fn(y)
            return carry

        if way == FORWARD:
            lax.fori_loop(me_y + 1, ny, body, 0)
        else:
            lax.fori_loop(0, me_y, body, 0)

    def z_from(way, part_at, i):
        src = lax.rem(me_z + ring_offset(i, nz), nz)
        chunk = way * HALVES + part_at
        return pltpu.make_async_remote_copy(
            states.at[way, pl.ds(0, half)],
            rec_z.at[way, part_at, src],
            z_send.at[chunk, src],
            z_recv.at[chunk, src],
            at_z(src),
            MESH,
        )

    def scan_row(way, part_at):
        over(nz - 1, lambda i: z_from(way, part_at, i).wait_recv())
        state = jnp.zeros((half, width), F32)
        for z in range(nz) if way == FORWARD else reversed(range(nz)):
            pre[way, part_at, z] = state
            state = state * dec_z[z] + rec_z[way, part_at, z]
        total[way, part_at] = state
        y_targets(way, lambda y: y_copy(way, part_at, y).start())

    def ret_copy(way, part_at, i):
        to = lax.rem(me_z + ring_offset(i, nz), nz)
        chunk = way * HALVES + part_at
        return pltpu.make_async_remote_copy(
            back.at[way, part_at, to],
            ret.at[way, part_at, me_z],
            r_send.at[chunk, to],
            r_recv.at[chunk, me_z],
            at_z(to),
            MESH,
        )

    def ret_from(way, part_at, i):
        src = lax.rem(me_z + ring_offset(i, nz), nz)
        chunk = way * HALVES + part_at
        return pltpu.make_async_remote_copy(
            back.at[way, part_at, src],
            ret.at[way, part_at, src],
            r_send.at[chunk, src],
            r_recv.at[chunk, src],
            at_z(src),
            MESH,
        )

    def carry_row(way, part_at):
        def body(i, state):
            y = i if way == FORWARD else ny - 1 - i
            y_from(way, part_at, y).wait_recv()
            return state * dec_y[y] + rec_y[way, part_at, y]

        steps = me_y if way == FORWARD else ny - 1 - me_y
        state = lax.fori_loop(0, steps, body, jnp.zeros((half, width), F32))
        for z in range(nz):
            back[way, part_at, z] = pre[way, part_at, z] + edge[way, z] * state
        over(nz - 1, lambda i: ret_copy(way, part_at, i).start())
        ret[way, part_at, me_z] = back[way, part_at, me_z]

    scan_row(FORWARD, 0)
    scan_row(FORWARD, 1)

    def wait_dec_y(i):
        src = lax.rem(me_y + ring_offset(i, ny), ny)
        pltpu.make_async_remote_copy(
            own_row, dec_y.at[src], dy_send.at[src], dy_recv.at[src], at_y(src), MESH
        ).wait_recv()

    over(ny - 1, wait_dec_y)
    carry_row(FORWARD, 0)
    scan_row(BACKWARD, 0)
    carry_row(FORWARD, 1)
    scan_row(BACKWARD, 1)
    carry_row(BACKWARD, 0)
    carry_row(BACKWARD, 1)

    def collect(way):
        for part_at in range(HALVES):
            over(nz - 1, lambda i: ret_from(way, part_at, i).wait_recv())
        for z in range(nz):
            both = jnp.concatenate([ret[way, part_at, z] for part_at in range(HALVES)], axis=0)
            hbf[way, z * piece : z * piece + piece] = both.astype(BF16)

    def t_copy(way, i):
        to = lax.rem(me_t + 1 + i, nt)
        return pltpu.make_async_remote_copy(
            part.at[way, pl.ds(pl.multiple_of(to * rows, rows), rows)],
            rec_t.at[way, me_t],
            t_send.at[way, to],
            t_recv.at[way, me_t],
            at_t(to),
            MESH,
        )

    def t_from(way, i):
        src = lax.rem(me_t + 1 + i, nt)
        return pltpu.make_async_remote_copy(
            part.at[way, pl.ds(0, rows)],
            rec_t.at[way, src],
            t_send.at[way, src],
            t_recv.at[way, src],
            at_t(src),
            MESH,
        )

    def share(way):
        over(nt - 1, lambda i: t_copy(way, i).start())
        rec_t[way, me_t] = part[way, pl.ds(pl.multiple_of(me_t * rows, rows), rows)]

    collect(FORWARD)
    part[0] += lax.dot_general(gw_v[...], hbf[FORWARD], NT, preferred_element_type=F32)
    share(0)
    collect(BACKWARD)
    part[1] += lax.dot_general(xw_v[...], hbf[BACKWARD], NT, preferred_element_type=F32)
    share(1)
    inter = jnp.dot(b_v[...], hbf[BACKWARD], preferred_element_type=F32)
    gx_bf[...] = (gx_acc[...] + tail_v[...] * inter).astype(BF16)
    store = pltpu.make_async_copy(gx_bf, gx_hbm, out_sem)
    store.start()

    for way, out in ((0, gc_out), (1, gb_out)):
        over(nt - 1, lambda i: t_from(way, i).wait_recv())
        out[...] = jnp.sum(rec_t[way], axis=0)

    over(nz - 1, lambda i: dec_z_copy(i).wait_send())
    over(ny - 1, lambda i: dec_y_copy(i).wait_send())
    for way in (FORWARD, BACKWARD):
        for part_at in range(HALVES):
            over(nz - 1, lambda i: z_copy(way, part_at, i).wait_send())
            y_targets(way, lambda y: y_copy(way, part_at, y).wait_send())
            over(nz - 1, lambda i: ret_copy(way, part_at, i).wait_send())
    for way in range(2):
        over(nt - 1, lambda i: t_copy(way, i).wait_send())
    store.wait()


def shards(x_heads, log_decay, b_proj, c_proj, grad_out):
    blocks, nt = lax.axis_size("ctx"), lax.axis_size("tp")
    ny, nz = grid_of(blocks)
    heads = log_decay.shape[0]
    width = heads * HEADDIM
    piece = STATE // nz
    half = piece // HALVES
    rows = GROUP // nt
    chunks = 2 * HALVES
    anywhere = pl.BlockSpec(memory_space=pl.ANY)
    in_vmem = pl.BlockSpec(memory_space=pltpu.VMEM)
    dma = pltpu.SemaphoreType.DMA
    vmem = pltpu.VMEM
    grad_x, grad_b, grad_c = pl.pallas_call(
        functools.partial(kernel, ny, nz, nt),
        out_shape=(
            jax.ShapeDtypeStruct((GROUP, width), BF16),
            jax.ShapeDtypeStruct((rows, STATE), F32),
            jax.ShapeDtypeStruct((rows, STATE), F32),
        ),
        in_specs=[anywhere] * 5,
        out_specs=(anywhere, in_vmem, in_vmem),
        scratch_shapes=[
            vmem((GROUP, width), BF16),
            vmem((heads, GROUP), F32),
            vmem((GROUP, STATE), BF16),
            vmem((GROUP, STATE), BF16),
            vmem((GROUP, width), BF16),
            vmem((GROUP, width), BF16),
            vmem((GROUP, width), BF16),
            vmem((GROUP, width), F32),
            vmem((heads, GROUP, 128), F32),
            vmem((heads, GROUP), F32),
            vmem((1, width), F32),
            vmem((nz, 1, width), F32),
            vmem((ny, 1, width), F32),
            vmem((1, width), F32),
            vmem((2, nz, 1, width), F32),
            vmem((2, STATE, width), F32),
            vmem((2, HALVES, nz, half, width), F32),
            vmem((2, HALVES, nz, half, width), F32),
            vmem((2, HALVES, half, width), F32),
            vmem((2, HALVES, ny, half, width), F32),
            vmem((2, HALVES, nz, half, width), F32),
            vmem((2, HALVES, nz, half, width), F32),
            vmem((2, STATE, width), BF16),
            vmem((GROUP, GROUP), F32),
            vmem((GROUP, width), F32),
            vmem((GROUP, width), BF16),
            vmem((2, GROUP, STATE), F32),
            vmem((2, nt, rows, STATE), F32),
            dma((5,)),
            dma,
            dma((nz,)),
            dma((nz,)),
            dma((ny,)),
            dma((ny,)),
            dma((chunks, nz)),
            dma((chunks, nz)),
            dma((chunks, ny)),
            dma((chunks, ny)),
            dma((chunks, nz)),
            dma((chunks, nz)),
            dma((2, nt)),
            dma((2, nt)),
        ],
        compiler_params=pltpu.CompilerParams(
            collective_id=0, has_side_effects=True, vmem_limit_bytes=48 * 1024 * 1024
        ),
        name="mixer_backward",
    )(x_heads, log_decay, b_proj, c_proj, grad_out)
    return grad_x, grad_b, grad_c


def solution(mesh):
    in_specs = (P("ctx", "tp"), P("tp", "ctx"), P("ctx", None), P("ctx", None), P("ctx", "tp"))
    out_specs = (P("ctx", "tp"), P(("ctx", "tp"), None), P(("ctx", "tp"), None))
    return jax.shard_map(shards, mesh=mesh, in_specs=in_specs, out_specs=out_specs, check_vma=False)
```

```python
import functools

import jax
import jax.numpy as jnp
from jax import lax
from jax.experimental import pallas as pl
from jax.experimental.pallas import tpu as pltpu
from jax.sharding import PartitionSpec as P

HEADDIM = 64
STATE = 128
GROUP = 256
HALVES = 2
FORWARD, BACKWARD = 0, 1
MESH = pl.DeviceIdType.MESH
F32, BF16 = jnp.float32, jnp.bfloat16
NT = (((1,), (1,)), ((), ()))


def grid_of(blocks):
    rows = 1
    while rows * rows < blocks:
        rows *= 2
    return blocks // rows, rows


def ring_offsets(size):
    return [size // 2 + ((i + 1) // 2) * (2 * (i % 2) - 1) for i in range(size - 1)]


def wait_bytes(ref, sem):
    pltpu.make_async_copy(ref, ref, sem).wait()


def kernel(
    ny, nz, nt,
    x_hbm, ld_hbm, b_hbm, c_hbm, g_hbm,
    gx_out, gb_out, gc_out,
    x_v, ld_v, b_v, c_v, g_v, xw_v, gw_v, tail_v, cols_v, row_v,
    own_dec, dec_z, dec_y, own_row, edge,
    states, rec_z, pre, total, rec_y, back, ret, hbf,
    acc_f, gx_acc, part, rec_t,
    load_sem,
    dz_send, dz_recv, dy_send, dy_recv, z_send, z_recv, y_send, y_recv, r_send, r_recv, t_send, t_recv,
):
    heads = ld_v.shape[0]
    width = x_v.shape[1]
    pairs = width // 128
    piece = STATE // nz
    half = piece // HALVES
    rows = GROUP // nt
    me = lax.axis_index("ctx")
    me_t = lax.axis_index("tp")
    me_y, me_z = me // nz, lax.rem(me, nz)

    def at_z(z):
        return {"ctx": me_y * nz + z}

    def at_y(y):
        return {"ctx": y * nz + me_z}

    def at_t(t):
        return {"tp": t}

    loads = [
        pltpu.make_async_copy(src, dst, load_sem.at[i])
        for i, (src, dst) in enumerate(
            ((ld_hbm, ld_v), (b_hbm, b_v), (x_hbm, x_v), (c_hbm, c_v), (g_hbm, g_v))
        )
    ]
    for load in loads:
        load.start()

    barrier = pltpu.get_barrier_semaphore()

    z_to = [lax.rem(me_z + off, nz) for off in ring_offsets(nz)]
    z_up = [k + jnp.where(me_z <= k, 1, 0) for k in range(nz - 1)]
    y_to = [lax.rem(me_y + off, ny) for off in ring_offsets(ny)]
    t_to = [lax.rem(me_t + off, nt) for off in range(1, nt)]
    for to, peers in ((at_z, z_to), (at_y, y_to), (at_t, t_to)):
        for peer in peers:
            pl.semaphore_signal(barrier, inc=1, device_id=to(peer), device_id_type=MESH)

    loads[0].wait()
    ld = ld_v[...]
    at_r = lax.broadcasted_iota(jnp.int32, (GROUP, GROUP), 0)
    at_c = lax.broadcasted_iota(jnp.int32, (GROUP, GROUP), 1)
    lower = (at_r >= at_c).astype(F32)
    high = lax.Precision.HIGHEST
    cum_t = lax.dot_general(lower, ld, NT, precision=high, preferred_element_type=F32)
    lane = lax.broadcasted_iota(jnp.int32, (GROUP, 128), 1)
    left = lane < HEADDIM
    for h in range(heads):
        cols_v[h] = jnp.broadcast_to(cum_t[:, h : h + 1], (GROUP, 128))

    loads[1].wait()
    loads[2].wait()
    for p in range(pairs):
        at = slice(p * 128, p * 128 + 128)
        cum = jnp.where(left, cols_v[2 * p], cols_v[2 * p + 1])
        last = cum[GROUP - 1 : GROUP, :]
        tail = jnp.exp(last - cum)
        tail_v[:, at] = tail
        xw_v[:, at] = (x_v[:, at].astype(F32) * tail).astype(BF16)
        own_dec[:, at] = jnp.exp(last)
    bt = b_v[...].astype(F32).T.astype(BF16)
    states[FORWARD] = jnp.dot(bt, xw_v[...], preferred_element_type=F32)

    pl.semaphore_wait(barrier, nz + ny + nt - 3)

    def remote(src, dst, send, recv, to):
        return pltpu.make_async_remote_copy(src, dst, send, recv, to, MESH)

    for to in z_to:
        remote(own_dec, dec_z.at[me_z], dz_send, dz_recv, at_z(to)).start()

    def send_pieces(way):
        for part_at in range(HALVES):
            chunk = way * HALVES + part_at
            for to in z_to:
                remote(
                    states.at[way, pl.ds(pl.multiple_of(to * piece + part_at * half, half), half)],
                    rec_z.at[way, part_at, me_z],
                    z_send.at[chunk],
                    z_recv.at[chunk],
                    at_z(to),
                ).start()
        for part_at in range(HALVES):
            rec_z[way, part_at, me_z] = states[
                way, pl.ds(pl.multiple_of(me_z * piece + part_at * half, half), half)
            ]

    send_pieces(FORWARD)
    dec_z[me_z] = own_dec[...]

    loads[3].wait()
    loads[4].wait()
    for p in range(pairs):
        at = slice(p * 128, p * 128 + 128)
        cum = jnp.where(left, cols_v[2 * p], cols_v[2 * p + 1])
        gw_v[:, at] = (g_v[:, at].astype(F32) * jnp.exp(cum)).astype(BF16)
    ct = c_v[...].astype(F32).T.astype(BF16)
    states[BACKWARD] = jnp.dot(ct, gw_v[...], preferred_element_type=F32)
    send_pieces(BACKWARD)

    others_z, others_y, others_t = pl.ds(0, nz - 1), pl.ds(0, ny - 1), pl.ds(0, nt - 1)
    wait_bytes(dec_z.at[others_z], dz_recv)
    ahead = jnp.ones((1, width), F32)
    for z in range(nz):
        edge[FORWARD, z] = ahead
        ahead = ahead * dec_z[z]
    own_row[...] = ahead
    behind = jnp.ones((1, width), F32)
    for z in reversed(range(nz)):
        edge[BACKWARD, z] = behind
        behind = behind * dec_z[z]
    for to in y_to:
        remote(own_row, dec_y.at[me_y], dy_send, dy_recv, at_y(to)).start()

    upper = (at_r <= at_c).astype(F32)
    row_v[...] = jnp.dot(ld, upper, precision=high, preferred_element_type=F32)
    gram_t = lax.dot_general(b_v[...], c_v[...], NT, preferred_element_type=F32)
    hb = GROUP // 2
    tri = (
        lax.broadcasted_iota(jnp.int32, (hb, hb), 0) <= lax.broadcasted_iota(jnp.int32, (hb, hb), 1)
    )
    lane_b = lax.broadcasted_iota(jnp.int32, (1, 128), 1)
    sides = ((lane_b < HEADDIM).astype(BF16), (lane_b >= HEADDIM).astype(BF16))
    tiles = ((0, 0), (0, 1), (1, 1))
    for p in range(pairs):
        at = slice(p * 128, p * 128 + 128)
        xp, gp = x_v[:, at], g_v[:, at]
        out = [jnp.zeros((hb, 128), F32) for _ in range(2)]
        for side in range(2):
            h = 2 * p + side
            gm = gp * sides[side]
            for ib, ub in tiles:
                mi, mu = slice(ib * hb, ib * hb + hb), slice(ub * hb, ub * hb + hb)
                mixed_t = lax.dot_general(xp[mi], gm[mu], NT, preferred_element_type=F32)
                decay_t = jnp.exp(jnp.minimum(row_v[h : h + 1, mu] - cols_v[h, mi, :], 0.0))
                if ib == ub:
                    decay_t = jnp.where(tri, decay_t, 0.0)
                first_t = mixed_t * decay_t
                if h == 0:
                    acc_f[mi, mu] = first_t
                else:
                    acc_f[mi, mu] += first_t
                third_t = (gram_t[mi, mu] * decay_t).astype(BF16)
                out[ib] = out[ib] + jnp.dot(third_t, gm[mu], preferred_element_type=F32)
        gx_acc[:hb, at] = out[0]
        gx_acc[hb:, at] = out[1]
    acc_f[hb:, :hb] = jnp.zeros((hb, hb), F32)
    first_t = acc_f[...]
    part[1] = jnp.dot(first_t.astype(BF16), c_v[...], preferred_element_type=F32)
    part[0] = jnp.dot(first_t.T.astype(BF16), b_v[...], preferred_element_type=F32)

    def y_copy(way, part_at, y):
        chunk = way * HALVES + part_at
        return remote(
            total.at[way, part_at],
            rec_y.at[way, part_at, me_y],
            y_send.at[chunk, y],
            y_recv.at[chunk, me_y],
            at_y(y),
        )

    def y_from(way, part_at, y):
        chunk = way * HALVES + part_at
        return remote(
            total.at[way, part_at],
            rec_y.at[way, part_at, y],
            y_send.at[chunk, y],
            y_recv.at[chunk, y],
            at_y(y),
        )

    def y_targets(way, fn):
        def body(y, carry):
            fn(y)
            return carry

        if way == FORWARD:
            lax.fori_loop(me_y + 1, ny, body, 0)
        else:
            lax.fori_loop(0, me_y, body, 0)

    def scan_row(way, part_at):
        wait_bytes(rec_z.at[way, part_at, others_z], z_recv.at[way * HALVES + part_at])
        state = jnp.zeros((half, width), F32)
        for z in range(nz) if way == FORWARD else reversed(range(nz)):
            pre[way, part_at, z] = state
            state = state * dec_z[z] + rec_z[way, part_at, z]
        total[way, part_at] = state
        y_targets(way, lambda y: y_copy(way, part_at, y).start())

    def carry_row(way, part_at):
        def body(i, state):
            y = i if way == FORWARD else ny - 1 - i
            y_from(way, part_at, y).wait_recv()
            return state * dec_y[y] + rec_y[way, part_at, y]

        steps = me_y if way == FORWARD else ny - 1 - me_y
        state = lax.fori_loop(0, steps, body, jnp.zeros((half, width), F32))
        for z in range(nz):
            back[way, part_at, z] = pre[way, part_at, z] + edge[way, z] * state
        ret[way, part_at, me_z] = back[way, part_at, me_z]

    def give_back(way, part_at, targets):
        chunk = way * HALVES + part_at
        for to in targets:
            remote(
                back.at[way, part_at, to],
                ret.at[way, part_at, me_z],
                r_send.at[chunk],
                r_recv.at[chunk],
                at_z(to),
            ).start()

    cut = (nz - 1) // 2
    early, late = z_up[:cut], z_up[cut:]
    scan_row(FORWARD, 0)
    scan_row(FORWARD, 1)
    wait_bytes(dec_y.at[others_y], dy_recv)
    carry_row(FORWARD, 0)
    give_back(FORWARD, 0, early)
    scan_row(BACKWARD, 0)
    carry_row(FORWARD, 1)
    give_back(FORWARD, 1, early)
    give_back(FORWARD, 0, late)
    scan_row(BACKWARD, 1)
    carry_row(BACKWARD, 0)
    give_back(BACKWARD, 0, early)
    give_back(FORWARD, 1, late)
    carry_row(BACKWARD, 1)
    give_back(BACKWARD, 1, early)
    give_back(BACKWARD, 0, late)
    give_back(BACKWARD, 1, late)

    def collect(way):
        for part_at in range(HALVES):
            wait_bytes(ret.at[way, part_at, others_z], r_recv.at[way * HALVES + part_at])
        for z in range(nz):
            both = jnp.concatenate([ret[way, part_at, z] for part_at in range(HALVES)], axis=0)
            hbf[way, z * piece : z * piece + piece] = both.astype(BF16)

    def share(way):
        for to in t_to:
            remote(
                part.at[way, pl.ds(pl.multiple_of(to * rows, rows), rows)],
                rec_t.at[way, me_t],
                t_send.at[way],
                t_recv.at[way],
                at_t(to),
            ).start()
        rec_t[way, me_t] = part[way, pl.ds(pl.multiple_of(me_t * rows, rows), rows)]

    collect(FORWARD)
    part[0] += lax.dot_general(gw_v[...], hbf[FORWARD], NT, preferred_element_type=F32)
    share(0)
    collect(BACKWARD)
    part[1] += lax.dot_general(xw_v[...], hbf[BACKWARD], NT, preferred_element_type=F32)
    share(1)
    inter = jnp.dot(b_v[...], hbf[BACKWARD], preferred_element_type=F32)
    gx_out[...] = (gx_acc[...] + tail_v[...] * inter).astype(BF16)

    wait_bytes(dec_z.at[others_z], dz_send)
    wait_bytes(dec_y.at[others_y], dy_send)
    for way in (FORWARD, BACKWARD):
        for part_at in range(HALVES):
            chunk = way * HALVES + part_at
            wait_bytes(rec_z.at[way, part_at, others_z], z_send.at[chunk])
            wait_bytes(ret.at[way, part_at, others_z], r_send.at[chunk])
            y_targets(way, lambda y: y_copy(way, part_at, y).wait_send())
    for way, out in ((0, gc_out), (1, gb_out)):
        wait_bytes(rec_t.at[way, others_t], t_recv.at[way])
        out[...] = jnp.sum(rec_t[way], axis=0)
        wait_bytes(rec_t.at[way, others_t], t_send.at[way])


def write_kernel(gx, gb, gc, gx_hbm, gb_hbm, gc_hbm, sem):
    copies = [
        pltpu.make_async_copy(src, dst, sem.at[i])
        for i, (src, dst) in enumerate(((gx, gx_hbm), (gb, gb_hbm), (gc, gc_hbm)))
    ]
    for copy in copies:
        copy.start()
    for copy in copies:
        copy.wait()


def shards(x_heads, log_decay, b_proj, c_proj, grad_out):
    blocks, nt = lax.axis_size("ctx"), lax.axis_size("tp")
    ny, nz = grid_of(blocks)
    heads = log_decay.shape[0]
    width = heads * HEADDIM
    piece = STATE // nz
    half = piece // HALVES
    rows = GROUP // nt
    chunks = 2 * HALVES
    in_hbm = pl.BlockSpec(memory_space=pltpu.HBM)
    in_vmem = pl.BlockSpec(memory_space=pltpu.VMEM)
    dma = pltpu.SemaphoreType.DMA
    vmem = pltpu.VMEM
    inputs = (x_heads, log_decay, b_proj, c_proj, grad_out)
    inputs = [pltpu.with_memory_space_constraint(a, pltpu.HBM) for a in inputs]
    out_shape = (
        jax.ShapeDtypeStruct((GROUP, width), BF16),
        jax.ShapeDtypeStruct((rows, STATE), F32),
        jax.ShapeDtypeStruct((rows, STATE), F32),
    )
    results = pl.pallas_call(
        functools.partial(kernel, ny, nz, nt),
        out_shape=out_shape,
        in_specs=[in_hbm] * 5,
        out_specs=[in_vmem] * 3,
        scratch_shapes=[
            vmem((GROUP, width), BF16),
            vmem((heads, GROUP), F32),
            vmem((GROUP, STATE), BF16),
            vmem((GROUP, STATE), BF16),
            vmem((GROUP, width), BF16),
            vmem((GROUP, width), BF16),
            vmem((GROUP, width), BF16),
            vmem((GROUP, width), F32),
            vmem((heads, GROUP, 128), F32),
            vmem((heads, GROUP), F32),
            vmem((1, width), F32),
            vmem((nz, 1, width), F32),
            vmem((ny, 1, width), F32),
            vmem((1, width), F32),
            vmem((2, nz, 1, width), F32),
            vmem((2, STATE, width), F32),
            vmem((2, HALVES, nz, half, width), F32),
            vmem((2, HALVES, nz, half, width), F32),
            vmem((2, HALVES, half, width), F32),
            vmem((2, HALVES, ny, half, width), F32),
            vmem((2, HALVES, nz, half, width), F32),
            vmem((2, HALVES, nz, half, width), F32),
            vmem((2, STATE, width), BF16),
            vmem((GROUP, GROUP), F32),
            vmem((GROUP, width), F32),
            vmem((2, GROUP, STATE), F32),
            vmem((2, nt, rows, STATE), F32),
            dma((5,)),
            dma,
            dma,
            dma,
            dma,
            dma((chunks,)),
            dma((chunks,)),
            dma((chunks, ny)),
            dma((chunks, ny)),
            dma((chunks,)),
            dma((chunks,)),
            dma((2,)),
            dma((2,)),
        ],
        compiler_params=pltpu.CompilerParams(
            collective_id=0, has_side_effects=True, vmem_limit_bytes=48 * 1024 * 1024
        ),
        name="mixer_backward",
    )(*inputs)
    return pl.pallas_call(
        write_kernel,
        out_shape=out_shape,
        in_specs=[pl.BlockSpec(memory_space=pl.ANY)] * 3,
        out_specs=[in_hbm] * 3,
        scratch_shapes=[dma((3,))],
        compiler_params=pltpu.CompilerParams(vmem_limit_bytes=1024 * 1024),
        name="write_out",
    )(*results)


def solution(mesh):
    in_specs = (P("ctx", "tp"), P("tp", "ctx"), P("ctx", None), P("ctx", None), P("ctx", "tp"))
    out_specs = (P("ctx", "tp"), P(("ctx", "tp"), None), P(("ctx", "tp"), None))
    return jax.shard_map(shards, mesh=mesh, in_specs=in_specs, out_specs=out_specs, check_vma=False)
```

```python
import functools

import jax
import jax.numpy as jnp
from jax import lax
from jax.experimental import pallas as pl
from jax.experimental.pallas import tpu as pltpu
from jax.sharding import PartitionSpec as P

HEADDIM = 64
STATE = 128
GROUP = 256
HALVES = 2
FORWARD, BACKWARD = 0, 1
MESH = pl.DeviceIdType.MESH
F32, BF16 = jnp.float32, jnp.bfloat16
NT = (((1,), (1,)), ((), ()))


def grid_of(blocks):
    rows = 1
    while rows * rows < blocks:
        rows *= 2
    return blocks // rows, rows


def ring_offsets(size):
    return [size // 2 + ((i + 1) // 2) * (2 * (i % 2) - 1) for i in range(size - 1)]


def wait_bytes(ref, sem):
    pltpu.make_async_copy(ref, ref, sem).wait()


def kernel(
    ny, nz, nt,
    x_hbm, ld_hbm, b_hbm, c_hbm, g_hbm,
    gx_out, gb_out, gc_out,
    x_v, ld_v, b_v, c_v, g_v, xw_v, gw_v, tail_v, cols_v, row_v,
    own_dec, dec_z, dec_y, own_row, edge,
    states, rec_z, pre, total, rec_y, back, ret, hbf,
    acc_f, gx_acc, part, rec_t,
    load_sem,
    dz_send, dz_recv, dy_send, dy_recv, z_send, z_recv, y_send, y_recv, r_send, r_recv, t_send, t_recv,
):
    heads = ld_v.shape[0]
    width = x_v.shape[1]
    pairs = width // 128
    piece = STATE // nz
    half = piece // HALVES
    rows = GROUP // nt
    me = lax.axis_index("ctx")
    me_t = lax.axis_index("tp")
    me_y, me_z = me // nz, lax.rem(me, nz)

    def at_z(z):
        return {"ctx": me_y * nz + z}

    def at_y(y):
        return {"ctx": y * nz + me_z}

    def at_t(t):
        return {"tp": t}

    loads = [
        pltpu.make_async_copy(src, dst, load_sem.at[i])
        for i, (src, dst) in enumerate(
            ((ld_hbm, ld_v), (b_hbm, b_v), (x_hbm, x_v), (c_hbm, c_v), (g_hbm, g_v))
        )
    ]
    for load in loads:
        load.start()

    barrier = pltpu.get_barrier_semaphore()

    z_to = [lax.rem(me_z + off, nz) for off in ring_offsets(nz)]
    z_up = [k + jnp.where(me_z <= k, 1, 0) for k in range(nz - 1)]
    y_to = [lax.rem(me_y + off, ny) for off in ring_offsets(ny)]
    t_to = [lax.rem(me_t + off, nt) for off in ring_offsets(nt)]
    for to, peers in ((at_z, z_to), (at_y, y_to), (at_t, t_to)):
        for peer in peers:
            pl.semaphore_signal(barrier, inc=1, device_id=to(peer), device_id_type=MESH)

    loads[0].wait()
    ld = ld_v[...]
    at_r = lax.broadcasted_iota(jnp.int32, (GROUP, GROUP), 0)
    at_c = lax.broadcasted_iota(jnp.int32, (GROUP, GROUP), 1)
    lower = (at_r >= at_c).astype(BF16)
    top = ld.astype(BF16)
    rest = ld - top.astype(F32)
    middle = rest.astype(BF16)
    parts = (top, middle, (rest - middle.astype(F32)).astype(BF16))
    cum_t = sum(lax.dot_general(lower, q, NT, preferred_element_type=F32) for q in parts)
    lane = lax.broadcasted_iota(jnp.int32, (GROUP, 128), 1)
    left = lane < HEADDIM
    for h in range(heads):
        cols_v[h] = jnp.broadcast_to(cum_t[:, h : h + 1], (GROUP, 128))

    loads[1].wait()
    loads[2].wait()
    for p in range(pairs):
        at = slice(p * 128, p * 128 + 128)
        cum = jnp.where(left, cols_v[2 * p], cols_v[2 * p + 1])
        last = cum[GROUP - 1 : GROUP, :]
        tail = jnp.exp(last - cum)
        tail_v[:, at] = tail
        xw_v[:, at] = (x_v[:, at].astype(F32) * tail).astype(BF16)
        own_dec[:, at] = jnp.exp(last)
    bt = b_v[...].astype(F32).T.astype(BF16)
    states[FORWARD] = jnp.dot(bt, xw_v[...], preferred_element_type=F32)

    pl.semaphore_wait(barrier, nz + ny + nt - 3)

    def remote(src, dst, send, recv, to):
        return pltpu.make_async_remote_copy(src, dst, send, recv, to, MESH)

    for to in z_to:
        remote(own_dec, dec_z.at[me_z], dz_send, dz_recv, at_z(to)).start()

    def send_pieces(way):
        for part_at in range(HALVES):
            chunk = way * HALVES + part_at
            for to in z_to:
                remote(
                    states.at[way, pl.ds(pl.multiple_of(to * piece + part_at * half, half), half)],
                    rec_z.at[way, part_at, me_z],
                    z_send.at[chunk],
                    z_recv.at[chunk],
                    at_z(to),
                ).start()
        for part_at in range(HALVES):
            rec_z[way, part_at, me_z] = states[
                way, pl.ds(pl.multiple_of(me_z * piece + part_at * half, half), half)
            ]

    send_pieces(FORWARD)
    dec_z[me_z] = own_dec[...]

    loads[3].wait()
    loads[4].wait()
    for p in range(pairs):
        at = slice(p * 128, p * 128 + 128)
        cum = jnp.where(left, cols_v[2 * p], cols_v[2 * p + 1])
        gw_v[:, at] = (g_v[:, at].astype(F32) * jnp.exp(cum)).astype(BF16)
    ct = c_v[...].astype(F32).T.astype(BF16)
    states[BACKWARD] = jnp.dot(ct, gw_v[...], preferred_element_type=F32)
    send_pieces(BACKWARD)

    others_z, others_y, others_t = pl.ds(0, nz - 1), pl.ds(0, ny - 1), pl.ds(0, nt - 1)
    wait_bytes(dec_z.at[others_z], dz_recv)
    ahead = jnp.ones((1, width), F32)
    for z in range(nz):
        edge[FORWARD, z] = ahead
        ahead = ahead * dec_z[z]
    own_row[...] = ahead
    behind = jnp.ones((1, width), F32)
    for z in reversed(range(nz)):
        edge[BACKWARD, z] = behind
        behind = behind * dec_z[z]
    for to in y_to:
        remote(own_row, dec_y.at[me_y], dy_send, dy_recv, at_y(to)).start()

    row_v[...] = sum(lax.dot_general(q, lower, NT, preferred_element_type=F32) for q in parts)
    gram_t = lax.dot_general(b_v[...], c_v[...], NT, preferred_element_type=F32)
    hb = GROUP // 2
    tri = (
        lax.broadcasted_iota(jnp.int32, (hb, hb), 0) <= lax.broadcasted_iota(jnp.int32, (hb, hb), 1)
    )
    lane_b = lax.broadcasted_iota(jnp.int32, (1, 128), 1)
    sides = ((lane_b < HEADDIM).astype(BF16), (lane_b >= HEADDIM).astype(BF16))
    tiles = ((0, 0), (0, 1), (1, 1))
    for p in range(pairs):
        at = slice(p * 128, p * 128 + 128)
        xp, gp = x_v[:, at], g_v[:, at]
        out = [jnp.zeros((hb, 128), F32) for _ in range(2)]
        for side in range(2):
            h = 2 * p + side
            gm = gp * sides[side]
            for ib, ub in tiles:
                mi, mu = slice(ib * hb, ib * hb + hb), slice(ub * hb, ub * hb + hb)
                mixed_t = lax.dot_general(xp[mi], gm[mu], NT, preferred_element_type=F32)
                decay_t = jnp.exp(jnp.minimum(row_v[h : h + 1, mu] - cols_v[h, mi, :], 0.0))
                if ib == ub:
                    decay_t = jnp.where(tri, decay_t, 0.0)
                first_t = mixed_t * decay_t
                if h == 0:
                    acc_f[mi, mu] = first_t
                else:
                    acc_f[mi, mu] += first_t
                third_t = (gram_t[mi, mu] * decay_t).astype(BF16)
                out[ib] = out[ib] + jnp.dot(third_t, gm[mu], preferred_element_type=F32)
        gx_acc[:hb, at] = out[0]
        gx_acc[hb:, at] = out[1]
    acc_f[hb:, :hb] = jnp.zeros((hb, hb), F32)
    first_t = acc_f[...]
    part[1] = jnp.dot(first_t.astype(BF16), c_v[...], preferred_element_type=F32)
    part[0] = jnp.dot(first_t.T.astype(BF16), b_v[...], preferred_element_type=F32)

    def y_copy(way, part_at, y):
        chunk = way * HALVES + part_at
        return remote(
            total.at[way, part_at],
            rec_y.at[way, part_at, me_y],
            y_send.at[chunk, y],
            y_recv.at[chunk, me_y],
            at_y(y),
        )

    def y_from(way, part_at, y):
        chunk = way * HALVES + part_at
        return remote(
            total.at[way, part_at],
            rec_y.at[way, part_at, y],
            y_send.at[chunk, y],
            y_recv.at[chunk, y],
            at_y(y),
        )

    def y_targets(way, fn):
        def body(y, carry):
            fn(y)
            return carry

        if way == FORWARD:
            lax.fori_loop(me_y + 1, ny, body, 0)
        else:
            lax.fori_loop(0, me_y, body, 0)

    def scan_row(way, part_at):
        wait_bytes(rec_z.at[way, part_at, others_z], z_recv.at[way * HALVES + part_at])
        state = jnp.zeros((half, width), F32)
        for z in range(nz) if way == FORWARD else reversed(range(nz)):
            pre[way, part_at, z] = state
            state = state * dec_z[z] + rec_z[way, part_at, z]
        total[way, part_at] = state
        y_targets(way, lambda y: y_copy(way, part_at, y).start())

    def carry_row(way, part_at):
        def body(i, state):
            y = i if way == FORWARD else ny - 1 - i
            y_from(way, part_at, y).wait_recv()
            return state * dec_y[y] + rec_y[way, part_at, y]

        steps = me_y if way == FORWARD else ny - 1 - me_y
        state = lax.fori_loop(0, steps, body, jnp.zeros((half, width), F32))
        for z in range(nz):
            back[way, part_at, z] = pre[way, part_at, z] + edge[way, z] * state
        ret[way, part_at, me_z] = back[way, part_at, me_z]

    def give_back(way, part_at, targets):
        chunk = way * HALVES + part_at
        for to in targets:
            remote(
                back.at[way, part_at, to],
                ret.at[way, part_at, me_z],
                r_send.at[chunk],
                r_recv.at[chunk],
                at_z(to),
            ).start()

    cut = (nz - 1) // 2
    early, late = z_up[:cut], z_up[cut:]
    scan_row(FORWARD, 0)
    scan_row(FORWARD, 1)
    wait_bytes(dec_y.at[others_y], dy_recv)
    carry_row(FORWARD, 0)
    give_back(FORWARD, 0, z_up)
    scan_row(BACKWARD, 0)
    carry_row(FORWARD, 1)
    give_back(FORWARD, 1, z_up)
    scan_row(BACKWARD, 1)
    carry_row(BACKWARD, 0)
    give_back(BACKWARD, 0, z_up[:1])
    carry_row(BACKWARD, 1)
    give_back(BACKWARD, 1, z_up[:1])
    give_back(BACKWARD, 0, z_up[1:])
    give_back(BACKWARD, 1, z_up[1:])

    def collect(way):
        for part_at in range(HALVES):
            wait_bytes(ret.at[way, part_at, others_z], r_recv.at[way * HALVES + part_at])
        for z in range(nz):
            both = jnp.concatenate([ret[way, part_at, z] for part_at in range(HALVES)], axis=0)
            hbf[way, z * piece : z * piece + piece] = both.astype(BF16)

    def share(way):
        for to in t_to:
            remote(
                part.at[way, pl.ds(pl.multiple_of(to * rows, rows), rows)],
                rec_t.at[way, me_t],
                t_send.at[way],
                t_recv.at[way],
                at_t(to),
            ).start()
        rec_t[way, me_t] = part[way, pl.ds(pl.multiple_of(me_t * rows, rows), rows)]

    collect(FORWARD)
    part[0] += lax.dot_general(gw_v[...], hbf[FORWARD], NT, preferred_element_type=F32)
    share(0)
    collect(BACKWARD)
    part[1] += lax.dot_general(xw_v[...], hbf[BACKWARD], NT, preferred_element_type=F32)
    share(1)
    inter = jnp.dot(b_v[...], hbf[BACKWARD], preferred_element_type=F32)
    gx_out[...] = (gx_acc[...] + tail_v[...] * inter).astype(BF16)

    wait_bytes(dec_z.at[others_z], dz_send)
    wait_bytes(dec_y.at[others_y], dy_send)
    for way in (FORWARD, BACKWARD):
        for part_at in range(HALVES):
            chunk = way * HALVES + part_at
            wait_bytes(rec_z.at[way, part_at, others_z], z_send.at[chunk])
            wait_bytes(ret.at[way, part_at, others_z], r_send.at[chunk])
            y_targets(way, lambda y: y_copy(way, part_at, y).wait_send())
    for way, out in ((0, gc_out), (1, gb_out)):
        wait_bytes(rec_t.at[way, others_t], t_recv.at[way])
        out[...] = jnp.sum(rec_t[way], axis=0)
        wait_bytes(rec_t.at[way, others_t], t_send.at[way])


def write_kernel(gx, gb, gc, gx_hbm, gb_hbm, gc_hbm, sem):
    copies = [
        pltpu.make_async_copy(src, dst, sem.at[i])
        for i, (src, dst) in enumerate(((gx, gx_hbm), (gb, gb_hbm), (gc, gc_hbm)))
    ]
    for copy in copies:
        copy.start()
    for copy in copies:
        copy.wait()


def shards(x_heads, log_decay, b_proj, c_proj, grad_out):
    blocks, nt = lax.axis_size("ctx"), lax.axis_size("tp")
    ny, nz = grid_of(blocks)
    heads = log_decay.shape[0]
    width = heads * HEADDIM
    piece = STATE // nz
    half = piece // HALVES
    rows = GROUP // nt
    chunks = 2 * HALVES
    in_hbm = pl.BlockSpec(memory_space=pltpu.HBM)
    in_vmem = pl.BlockSpec(memory_space=pltpu.VMEM)
    dma = pltpu.SemaphoreType.DMA
    vmem = pltpu.VMEM
    inputs = (x_heads, log_decay, b_proj, c_proj, grad_out)
    inputs = [pltpu.with_memory_space_constraint(a, pltpu.HBM) for a in inputs]
    out_shape = (
        jax.ShapeDtypeStruct((GROUP, width), BF16),
        jax.ShapeDtypeStruct((rows, STATE), F32),
        jax.ShapeDtypeStruct((rows, STATE), F32),
    )
    results = pl.pallas_call(
        functools.partial(kernel, ny, nz, nt),
        out_shape=out_shape,
        in_specs=[in_hbm] * 5,
        out_specs=[in_vmem] * 3,
        scratch_shapes=[
            vmem((GROUP, width), BF16),
            vmem((heads, GROUP), F32),
            vmem((GROUP, STATE), BF16),
            vmem((GROUP, STATE), BF16),
            vmem((GROUP, width), BF16),
            vmem((GROUP, width), BF16),
            vmem((GROUP, width), BF16),
            vmem((GROUP, width), F32),
            vmem((heads, GROUP, 128), F32),
            vmem((heads, GROUP), F32),
            vmem((1, width), F32),
            vmem((nz, 1, width), F32),
            vmem((ny, 1, width), F32),
            vmem((1, width), F32),
            vmem((2, nz, 1, width), F32),
            vmem((2, STATE, width), F32),
            vmem((2, HALVES, nz, half, width), F32),
            vmem((2, HALVES, nz, half, width), F32),
            vmem((2, HALVES, half, width), F32),
            vmem((2, HALVES, ny, half, width), F32),
            vmem((2, HALVES, nz, half, width), F32),
            vmem((2, HALVES, nz, half, width), F32),
            vmem((2, STATE, width), BF16),
            vmem((GROUP, GROUP), F32),
            vmem((GROUP, width), F32),
            vmem((2, GROUP, STATE), F32),
            vmem((2, nt, rows, STATE), F32),
            dma((5,)),
            dma,
            dma,
            dma,
            dma,
            dma((chunks,)),
            dma((chunks,)),
            dma((chunks, ny)),
            dma((chunks, ny)),
            dma((chunks,)),
            dma((chunks,)),
            dma((2,)),
            dma((2,)),
        ],
        compiler_params=pltpu.CompilerParams(
            collective_id=0, has_side_effects=True, vmem_limit_bytes=48 * 1024 * 1024
        ),
        name="mixer_backward",
    )(*inputs)
    return pl.pallas_call(
        write_kernel,
        out_shape=out_shape,
        in_specs=[pl.BlockSpec(memory_space=pl.ANY)] * 3,
        out_specs=[in_hbm] * 3,
        scratch_shapes=[dma((3,))],
        compiler_params=pltpu.CompilerParams(vmem_limit_bytes=1024 * 1024),
        name="write_out",
    )(*results)


def solution(mesh):
    in_specs = (P("ctx", "tp"), P("tp", "ctx"), P("ctx", None), P("ctx", None), P("ctx", "tp"))
    out_specs = (P("ctx", "tp"), P(("ctx", "tp"), None), P(("ctx", "tp"), None))
    return jax.shard_map(shards, mesh=mesh, in_specs=in_specs, out_specs=out_specs, check_vma=False)
```

```python
import functools

import jax
import jax.numpy as jnp
from jax import lax
from jax.experimental import pallas as pl
from jax.experimental.pallas import tpu as pltpu
from jax.sharding import PartitionSpec as P

HEADDIM = 64
STATE = 128
GROUP = 256
HALVES = 2
FORWARD, BACKWARD = 0, 1
MESH = pl.DeviceIdType.MESH
F32, BF16 = jnp.float32, jnp.bfloat16
NT = (((1,), (1,)), ((), ()))


def grid_of(blocks):
    rows = 1
    while rows * rows < blocks:
        rows *= 2
    return blocks // rows, rows


def ring_offsets(size):
    return [size // 2 + ((i + 1) // 2) * (2 * (i % 2) - 1) for i in range(size - 1)]


def wait_bytes(ref, sem):
    pltpu.make_async_copy(ref, ref, sem).wait()


def kernel(
    ny, nz, nt,
    x_hbm, ld_hbm, b_hbm, c_hbm, g_hbm,
    gx_out, gb_out, gc_out,
    x_v, ld_v, b_v, c_v, g_v, xw_v, gw_v, tail_v, cols_v, row_v,
    own_dec, dec_z, dec_y, own_row, edge,
    states, rec_z, pre, total, rec_y, back, ret, hbf,
    acc_f, gx_acc, part, rec_t,
    load_sem, row_in, rows_in,
    dz_send, dz_recv, dy_send, dy_recv, z_send, z_recv, y_send, y_recv, r_send, r_recv, t_send, t_recv,
):
    heads = ld_v.shape[0]
    width = x_v.shape[1]
    pairs = width // 128
    piece = STATE // nz
    half = piece // HALVES
    rows = GROUP // nt
    me = lax.axis_index("ctx")
    me_t = lax.axis_index("tp")
    me_y, me_z = me // nz, lax.rem(me, nz)

    def at_z(z):
        return {"ctx": me_y * nz + z}

    def at_y(y):
        return {"ctx": y * nz + me_z}

    def at_t(t):
        return {"tp": t}

    loads = [
        pltpu.make_async_copy(src, dst, load_sem.at[i])
        for i, (src, dst) in enumerate(
            ((ld_hbm, ld_v), (b_hbm, b_v), (x_hbm, x_v), (c_hbm, c_v), (g_hbm, g_v))
        )
    ]
    for load in loads:
        load.start()

    barrier = pltpu.get_barrier_semaphore()

    z_to = [lax.rem(me_z + off, nz) for off in ring_offsets(nz)]
    z_up = [k + jnp.where(me_z <= k, 1, 0) for k in range(nz - 1)]
    y_to = [lax.rem(me_y + off, ny) for off in ring_offsets(ny)]
    t_to = [lax.rem(me_t + off, nt) for off in ring_offsets(nt)]
    first = me_z == 0

    def signal(sem, to):
        pl.semaphore_signal(sem, inc=1, device_id=to, device_id_type=MESH)

    for peer in z_to:
        signal(barrier, at_z(peer))
    for peer in t_to:
        signal(barrier, at_t(peer))

    @pl.when(first)
    def _():
        for peer in y_to:
            signal(barrier, at_y(peer))

    loads[0].wait()
    ld = ld_v[...]
    at_r = lax.broadcasted_iota(jnp.int32, (GROUP, GROUP), 0)
    at_c = lax.broadcasted_iota(jnp.int32, (GROUP, GROUP), 1)
    lower = (at_r >= at_c).astype(BF16)
    top = ld.astype(BF16)
    rest = ld - top.astype(F32)
    middle = rest.astype(BF16)
    parts = (top, middle, (rest - middle.astype(F32)).astype(BF16))
    cum_t = sum(lax.dot_general(lower, q, NT, preferred_element_type=F32) for q in parts)
    lane = lax.broadcasted_iota(jnp.int32, (GROUP, 128), 1)
    left = lane < HEADDIM
    for h in range(heads):
        cols_v[h] = jnp.broadcast_to(cum_t[:, h : h + 1], (GROUP, 128))

    loads[1].wait()
    loads[2].wait()
    for p in range(pairs):
        at = slice(p * 128, p * 128 + 128)
        cum = jnp.where(left, cols_v[2 * p], cols_v[2 * p + 1])
        last = cum[GROUP - 1 : GROUP, :]
        tail = jnp.exp(last - cum)
        tail_v[:, at] = tail
        xw_v[:, at] = (x_v[:, at].astype(F32) * tail).astype(BF16)
        own_dec[:, at] = jnp.exp(last)
    bt = b_v[...].astype(F32).T.astype(BF16)
    states[FORWARD] = jnp.dot(bt, xw_v[...], preferred_element_type=F32)

    pl.semaphore_wait(barrier, nz + nt - 2 + jnp.where(first, ny - 1, 0))

    @pl.when(first)
    def _():
        for peer in y_to:
            signal(row_in, at_y(peer))


    def remote(src, dst, send, recv, to):
        return pltpu.make_async_remote_copy(src, dst, send, recv, to, MESH)

    for to in z_to:
        remote(own_dec, dec_z.at[me_z], dz_send, dz_recv, at_z(to)).start()

    def send_pieces(way, part_at):
        chunk = way * HALVES + part_at
        for to in z_to:
            remote(
                states.at[way, pl.ds(pl.multiple_of(to * piece + part_at * half, half), half)],
                rec_z.at[way, part_at, me_z],
                z_send.at[chunk],
                z_recv.at[chunk],
                at_z(to),
            ).start()

    def keep_own(way):
        for part_at in range(HALVES):
            rec_z[way, part_at, me_z] = states[
                way, pl.ds(pl.multiple_of(me_z * piece + part_at * half, half), half)
            ]

    send_pieces(FORWARD, 0)
    keep_own(FORWARD)
    dec_z[me_z] = own_dec[...]

    loads[3].wait()
    loads[4].wait()
    for p in range(pairs):
        at = slice(p * 128, p * 128 + 128)
        cum = jnp.where(left, cols_v[2 * p], cols_v[2 * p + 1])
        gw_v[:, at] = (g_v[:, at].astype(F32) * jnp.exp(cum)).astype(BF16)
    ct = c_v[...].astype(F32).T.astype(BF16)
    states[BACKWARD] = jnp.dot(ct, gw_v[...], preferred_element_type=F32)
    send_pieces(BACKWARD, 0)
    send_pieces(FORWARD, 1)
    send_pieces(BACKWARD, 1)
    keep_own(BACKWARD)

    others_z, others_y, others_t = pl.ds(0, nz - 1), pl.ds(0, ny - 1), pl.ds(0, nt - 1)
    wait_bytes(dec_z.at[others_z], dz_recv)
    ahead = jnp.ones((1, width), F32)
    for z in range(nz):
        edge[FORWARD, z] = ahead
        ahead = ahead * dec_z[z]
    own_row[...] = ahead
    behind = jnp.ones((1, width), F32)
    for z in reversed(range(nz)):
        edge[BACKWARD, z] = behind
        behind = behind * dec_z[z]

    row_v[...] = sum(lax.dot_general(q, lower, NT, preferred_element_type=F32) for q in parts)
    gram_t = lax.dot_general(b_v[...], c_v[...], NT, preferred_element_type=F32)
    hb = GROUP // 2
    tri = (
        lax.broadcasted_iota(jnp.int32, (hb, hb), 0) <= lax.broadcasted_iota(jnp.int32, (hb, hb), 1)
    )
    lane_b = lax.broadcasted_iota(jnp.int32, (1, 128), 1)
    sides = ((lane_b < HEADDIM).astype(BF16), (lane_b >= HEADDIM).astype(BF16))
    tiles = ((0, 0), (0, 1), (1, 1))
    for p in range(pairs):
        at = slice(p * 128, p * 128 + 128)
        xp, gp = x_v[:, at], g_v[:, at]
        out = [jnp.zeros((hb, 128), F32) for _ in range(2)]
        for side in range(2):
            h = 2 * p + side
            gm = gp * sides[side]
            for ib, ub in tiles:
                mi, mu = slice(ib * hb, ib * hb + hb), slice(ub * hb, ub * hb + hb)
                mixed_t = lax.dot_general(xp[mi], gm[mu], NT, preferred_element_type=F32)
                decay_t = jnp.exp(jnp.minimum(row_v[h : h + 1, mu] - cols_v[h, mi, :], 0.0))
                if ib == ub:
                    decay_t = jnp.where(tri, decay_t, 0.0)
                first_t = mixed_t * decay_t
                if h == 0:
                    acc_f[mi, mu] = first_t
                else:
                    acc_f[mi, mu] += first_t
                third_t = (gram_t[mi, mu] * decay_t).astype(BF16)
                out[ib] = out[ib] + jnp.dot(third_t, gm[mu], preferred_element_type=F32)
        gx_acc[:hb, at] = out[0]
        gx_acc[hb:, at] = out[1]
    acc_f[hb:, :hb] = jnp.zeros((hb, hb), F32)
    first_t = acc_f[...]
    part[1] = jnp.dot(first_t.astype(BF16), c_v[...], preferred_element_type=F32)
    part[0] = jnp.dot(first_t.T.astype(BF16), b_v[...], preferred_element_type=F32)

    @pl.when(first)
    def _():
        pl.semaphore_wait(row_in, ny - 1)
        for z in range(1, nz):
            signal(rows_in, at_z(z))

    pl.when(me_z > 0)(lambda: pl.semaphore_wait(rows_in, 1))
    for to in y_to:
        remote(own_row, dec_y.at[me_y], dy_send, dy_recv, at_y(to)).start()

    def y_copy(way, part_at, y):
        chunk = way * HALVES + part_at
        return remote(
            total.at[way, part_at],
            rec_y.at[way, part_at, me_y],
            y_send.at[chunk, y],
            y_recv.at[chunk, me_y],
            at_y(y),
        )

    def y_from(way, part_at, y):
        chunk = way * HALVES + part_at
        return remote(
            total.at[way, part_at],
            rec_y.at[way, part_at, y],
            y_send.at[chunk, y],
            y_recv.at[chunk, y],
            at_y(y),
        )

    def y_targets(way, fn):
        def body(y, carry):
            fn(y)
            return carry

        if way == FORWARD:
            lax.fori_loop(me_y + 1, ny, body, 0)
        else:
            lax.fori_loop(0, me_y, body, 0)

    def scan_row(way, part_at):
        wait_bytes(rec_z.at[way, part_at, others_z], z_recv.at[way * HALVES + part_at])
        state = jnp.zeros((half, width), F32)
        for z in range(nz) if way == FORWARD else reversed(range(nz)):
            pre[way, part_at, z] = state
            state = state * dec_z[z] + rec_z[way, part_at, z]
        total[way, part_at] = state
        y_targets(way, lambda y: y_copy(way, part_at, y).start())

    def carry_row(way, part_at):
        def body(i, state):
            y = i if way == FORWARD else ny - 1 - i
            y_from(way, part_at, y).wait_recv()
            return state * dec_y[y] + rec_y[way, part_at, y]

        steps = me_y if way == FORWARD else ny - 1 - me_y
        state = lax.fori_loop(0, steps, body, jnp.zeros((half, width), F32))
        for z in range(nz):
            back[way, part_at, z] = pre[way, part_at, z] + edge[way, z] * state
        ret[way, part_at, me_z] = back[way, part_at, me_z]

    def give_back(way, part_at, targets):
        chunk = way * HALVES + part_at
        for to in targets:
            remote(
                back.at[way, part_at, to],
                ret.at[way, part_at, me_z],
                r_send.at[chunk],
                r_recv.at[chunk],
                at_z(to),
            ).start()

    cut = (nz - 1) // 2
    early, late = z_up[:cut], z_up[cut:]
    scan_row(FORWARD, 0)
    scan_row(BACKWARD, 0)
    wait_bytes(dec_y.at[others_y], dy_recv)
    carry_row(FORWARD, 0)
    give_back(FORWARD, 0, z_up)
    scan_row(FORWARD, 1)
    carry_row(BACKWARD, 0)
    give_back(BACKWARD, 0, z_up)
    scan_row(BACKWARD, 1)
    carry_row(FORWARD, 1)
    give_back(FORWARD, 1, z_up[:2])
    carry_row(BACKWARD, 1)
    give_back(BACKWARD, 1, z_up[:2])
    give_back(FORWARD, 1, z_up[2:])
    give_back(BACKWARD, 1, z_up[2:])

    def collect(way):
        for part_at in range(HALVES):
            wait_bytes(ret.at[way, part_at, others_z], r_recv.at[way * HALVES + part_at])
        for z in range(nz):
            both = jnp.concatenate([ret[way, part_at, z] for part_at in range(HALVES)], axis=0)
            hbf[way, z * piece : z * piece + piece] = both.astype(BF16)

    def share(way):
        for to in t_to:
            remote(
                part.at[way, pl.ds(pl.multiple_of(to * rows, rows), rows)],
                rec_t.at[way, me_t],
                t_send.at[way],
                t_recv.at[way],
                at_t(to),
            ).start()
        rec_t[way, me_t] = part[way, pl.ds(pl.multiple_of(me_t * rows, rows), rows)]

    collect(FORWARD)
    part[0] += lax.dot_general(gw_v[...], hbf[FORWARD], NT, preferred_element_type=F32)
    share(0)
    collect(BACKWARD)
    part[1] += lax.dot_general(xw_v[...], hbf[BACKWARD], NT, preferred_element_type=F32)
    share(1)
    inter = jnp.dot(b_v[...], hbf[BACKWARD], preferred_element_type=F32)
    gx_out[...] = (gx_acc[...] + tail_v[...] * inter).astype(BF16)

    wait_bytes(dec_z.at[others_z], dz_send)
    wait_bytes(dec_y.at[others_y], dy_send)
    for way in (FORWARD, BACKWARD):
        for part_at in range(HALVES):
            chunk = way * HALVES + part_at
            wait_bytes(rec_z.at[way, part_at, others_z], z_send.at[chunk])
            wait_bytes(ret.at[way, part_at, others_z], r_send.at[chunk])
            y_targets(way, lambda y: y_copy(way, part_at, y).wait_send())
    for way, out in ((0, gc_out), (1, gb_out)):
        wait_bytes(rec_t.at[way, others_t], t_recv.at[way])
        out[...] = jnp.sum(rec_t[way], axis=0)
        wait_bytes(rec_t.at[way, others_t], t_send.at[way])


def write_kernel(gx, gb, gc, gx_hbm, gb_hbm, gc_hbm, sem):
    copies = [
        pltpu.make_async_copy(src, dst, sem.at[i])
        for i, (src, dst) in enumerate(((gx, gx_hbm), (gb, gb_hbm), (gc, gc_hbm)))
    ]
    for copy in copies:
        copy.start()
    for copy in copies:
        copy.wait()


def shards(x_heads, log_decay, b_proj, c_proj, grad_out):
    blocks, nt = lax.axis_size("ctx"), lax.axis_size("tp")
    ny, nz = grid_of(blocks)
    heads = log_decay.shape[0]
    width = heads * HEADDIM
    piece = STATE // nz
    half = piece // HALVES
    rows = GROUP // nt
    chunks = 2 * HALVES
    in_hbm = pl.BlockSpec(memory_space=pltpu.HBM)
    in_vmem = pl.BlockSpec(memory_space=pltpu.VMEM)
    dma = pltpu.SemaphoreType.DMA
    vmem = pltpu.VMEM
    inputs = (x_heads, log_decay, b_proj, c_proj, grad_out)
    inputs = [pltpu.with_memory_space_constraint(a, pltpu.HBM) for a in inputs]
    out_shape = (
        jax.ShapeDtypeStruct((GROUP, width), BF16),
        jax.ShapeDtypeStruct((rows, STATE), F32),
        jax.ShapeDtypeStruct((rows, STATE), F32),
    )
    results = pl.pallas_call(
        functools.partial(kernel, ny, nz, nt),
        out_shape=out_shape,
        in_specs=[in_hbm] * 5,
        out_specs=[in_vmem] * 3,
        scratch_shapes=[
            vmem((GROUP, width), BF16),
            vmem((heads, GROUP), F32),
            vmem((GROUP, STATE), BF16),
            vmem((GROUP, STATE), BF16),
            vmem((GROUP, width), BF16),
            vmem((GROUP, width), BF16),
            vmem((GROUP, width), BF16),
            vmem((GROUP, width), F32),
            vmem((heads, GROUP, 128), F32),
            vmem((heads, GROUP), F32),
            vmem((1, width), F32),
            vmem((nz, 1, width), F32),
            vmem((ny, 1, width), F32),
            vmem((1, width), F32),
            vmem((2, nz, 1, width), F32),
            vmem((2, STATE, width), F32),
            vmem((2, HALVES, nz, half, width), F32),
            vmem((2, HALVES, nz, half, width), F32),
            vmem((2, HALVES, half, width), F32),
            vmem((2, HALVES, ny, half, width), F32),
            vmem((2, HALVES, nz, half, width), F32),
            vmem((2, HALVES, nz, half, width), F32),
            vmem((2, STATE, width), BF16),
            vmem((GROUP, GROUP), F32),
            vmem((GROUP, width), F32),
            vmem((2, GROUP, STATE), F32),
            vmem((2, nt, rows, STATE), F32),
            dma((5,)),
            pltpu.SemaphoreType.REGULAR,
            pltpu.SemaphoreType.REGULAR,
            dma,
            dma,
            dma,
            dma,
            dma((chunks,)),
            dma((chunks,)),
            dma((chunks, ny)),
            dma((chunks, ny)),
            dma((chunks,)),
            dma((chunks,)),
            dma((2,)),
            dma((2,)),
        ],
        compiler_params=pltpu.CompilerParams(
            collective_id=0, has_side_effects=True, vmem_limit_bytes=48 * 1024 * 1024
        ),
        name="mixer_backward",
    )(*inputs)
    return pl.pallas_call(
        write_kernel,
        out_shape=out_shape,
        in_specs=[pl.BlockSpec(memory_space=pl.ANY)] * 3,
        out_specs=[in_hbm] * 3,
        scratch_shapes=[dma((3,))],
        compiler_params=pltpu.CompilerParams(vmem_limit_bytes=1024 * 1024),
        name="write_out",
    )(*results)


def solution(mesh):
    in_specs = (P("ctx", "tp"), P("tp", "ctx"), P("ctx", None), P("ctx", None), P("ctx", "tp"))
    out_specs = (P("ctx", "tp"), P(("ctx", "tp"), None), P(("ctx", "tp"), None))
    return jax.shard_map(shards, mesh=mesh, in_specs=in_specs, out_specs=out_specs, check_vma=False)
```

```python
import functools

import jax
import jax.numpy as jnp
from jax import lax
from jax.experimental import pallas as pl
from jax.experimental.pallas import tpu as pltpu
from jax.sharding import PartitionSpec as P

HEADDIM = 64
STATE = 128
GROUP = 256
HALVES = 2
FORWARD, BACKWARD = 0, 1
MESH = pl.DeviceIdType.MESH
F32, BF16 = jnp.float32, jnp.bfloat16
NT = (((1,), (1,)), ((), ()))


def grid_of(blocks):
    rows = 1
    while rows * rows < blocks:
        rows *= 2
    return blocks // rows, rows


def ring_offsets(size):
    return [size // 2 + ((i + 1) // 2) * (2 * (i % 2) - 1) for i in range(size - 1)]


def wait_bytes(ref, sem):
    pltpu.make_async_copy(ref, ref, sem).wait()


def kernel(
    ny, nz, nt,
    x_hbm, ld_hbm, b_hbm, c_hbm, g_hbm,
    gx_out, gb_out, gc_out,
    x_v, ld_v, b_v, c_v, g_v, xw_v, gw_v, tail_v, cols_v, row_v,
    own_dec, dec_z, dec_y, own_row, edge,
    states, rec_z, pre, total, rec_y, back, ret, hbf,
    acc_f, gx_acc, part, rec_t,
    load_sem, row_in, rows_in,
    dz_send, dz_recv, dy_send, dy_recv, z_send, z_recv, y_send, y_recv, r_send, r_recv, t_send, t_recv,
):
    heads = ld_v.shape[0]
    width = x_v.shape[1]
    pairs = width // 128
    piece = STATE // nz
    half = piece // HALVES
    rows = GROUP // nt
    me = lax.axis_index("ctx")
    me_t = lax.axis_index("tp")
    me_y, me_z = me // nz, lax.rem(me, nz)

    def at_z(z):
        return {"ctx": me_y * nz + z}

    def at_y(y):
        return {"ctx": y * nz + me_z}

    def at_t(t):
        return {"tp": t}

    loads = [
        pltpu.make_async_copy(src, dst, load_sem.at[i])
        for i, (src, dst) in enumerate(
            ((ld_hbm, ld_v), (b_hbm, b_v), (x_hbm, x_v), (c_hbm, c_v), (g_hbm, g_v))
        )
    ]
    for load in loads:
        load.start()

    barrier = pltpu.get_barrier_semaphore()

    z_to = [lax.rem(me_z + off, nz) for off in ring_offsets(nz)]
    z_up = [k + jnp.where(me_z <= k, 1, 0) for k in range(nz - 1)]
    y_to = [lax.rem(me_y + off, ny) for off in ring_offsets(ny)]
    t_to = [lax.rem(me_t + off, nt) for off in ring_offsets(nt)]
    first = me_z == 0

    def signal(sem, to):
        pl.semaphore_signal(sem, inc=1, device_id=to, device_id_type=MESH)

    for peer in z_to:
        signal(barrier, at_z(peer))
    for peer in t_to:
        signal(barrier, at_t(peer))

    @pl.when(first)
    def _():
        for peer in y_to:
            signal(barrier, at_y(peer))

    loads[0].wait()
    ld = ld_v[...]
    at_r = lax.broadcasted_iota(jnp.int32, (GROUP, GROUP), 0)
    at_c = lax.broadcasted_iota(jnp.int32, (GROUP, GROUP), 1)
    lower = (at_r >= at_c).astype(BF16)
    top = ld.astype(BF16)
    rest = ld - top.astype(F32)
    middle = rest.astype(BF16)
    parts = (top, middle, (rest - middle.astype(F32)).astype(BF16))
    cum_t = sum(lax.dot_general(lower, q, NT, preferred_element_type=F32) for q in parts)
    lane = lax.broadcasted_iota(jnp.int32, (GROUP, 128), 1)
    left = lane < HEADDIM
    for h in range(heads):
        cols_v[h] = jnp.broadcast_to(cum_t[:, h : h + 1], (GROUP, 128))

    loads[1].wait()
    loads[2].wait()
    for p in range(pairs):
        at = slice(p * 128, p * 128 + 128)
        cum = jnp.where(left, cols_v[2 * p], cols_v[2 * p + 1])
        last = cum[GROUP - 1 : GROUP, :]
        tail = jnp.exp(last - cum)
        tail_v[:, at] = tail
        xw_v[:, at] = (x_v[:, at].astype(F32) * tail).astype(BF16)
        own_dec[:, at] = jnp.exp(last)
    bt = b_v[...].astype(F32).T.astype(BF16)
    states[FORWARD] = jnp.dot(bt, xw_v[...], preferred_element_type=F32)

    pl.semaphore_wait(barrier, nz + nt - 2 + jnp.where(first, ny - 1, 0))

    @pl.when(first)
    def _():
        for peer in y_to:
            signal(row_in, at_y(peer))


    def remote(src, dst, send, recv, to):
        return pltpu.make_async_remote_copy(src, dst, send, recv, to, MESH)

    for to in z_to:
        remote(own_dec, dec_z.at[me_z], dz_send, dz_recv, at_z(to)).start()

    def send_pieces(way, part_at):
        chunk = way * HALVES + part_at
        for to in z_to:
            remote(
                states.at[way, pl.ds(pl.multiple_of(to * piece + part_at * half, half), half)],
                rec_z.at[way, part_at, me_z],
                z_send.at[chunk],
                z_recv.at[chunk],
                at_z(to),
            ).start()

    def keep_own(way):
        for part_at in range(HALVES):
            rec_z[way, part_at, me_z] = states[
                way, pl.ds(pl.multiple_of(me_z * piece + part_at * half, half), half)
            ]

    send_pieces(FORWARD, 0)
    keep_own(FORWARD)
    dec_z[me_z] = own_dec[...]

    loads[3].wait()
    loads[4].wait()
    for p in range(pairs):
        at = slice(p * 128, p * 128 + 128)
        cum = jnp.where(left, cols_v[2 * p], cols_v[2 * p + 1])
        gw_v[:, at] = (g_v[:, at].astype(F32) * jnp.exp(cum)).astype(BF16)
    ct = c_v[...].astype(F32).T.astype(BF16)
    states[BACKWARD] = jnp.dot(ct, gw_v[...], preferred_element_type=F32)
    send_pieces(BACKWARD, 0)
    send_pieces(FORWARD, 1)
    send_pieces(BACKWARD, 1)
    keep_own(BACKWARD)

    others_z, others_y, others_t = pl.ds(0, nz - 1), pl.ds(0, ny - 1), pl.ds(0, nt - 1)
    wait_bytes(dec_z.at[others_z], dz_recv)
    ahead = jnp.ones((1, width), F32)
    for z in range(nz):
        edge[FORWARD, z] = ahead
        ahead = ahead * dec_z[z]
    own_row[...] = ahead
    behind = jnp.ones((1, width), F32)
    for z in reversed(range(nz)):
        edge[BACKWARD, z] = behind
        behind = behind * dec_z[z]

    row_v[...] = sum(lax.dot_general(q, lower, NT, preferred_element_type=F32) for q in parts)
    gram_t = lax.dot_general(b_v[...], c_v[...], NT, preferred_element_type=F32)
    hb = GROUP // 2
    tri = (
        lax.broadcasted_iota(jnp.int32, (hb, hb), 0) <= lax.broadcasted_iota(jnp.int32, (hb, hb), 1)
    )
    lane_b = lax.broadcasted_iota(jnp.int32, (1, 128), 1)
    sides = ((lane_b < HEADDIM).astype(BF16), (lane_b >= HEADDIM).astype(BF16))
    tiles = ((0, 0), (0, 1), (1, 1))
    for p in range(pairs):
        at = slice(p * 128, p * 128 + 128)
        xp, gp = x_v[:, at], g_v[:, at]
        out = [jnp.zeros((hb, 128), F32) for _ in range(2)]
        for side in range(2):
            h = 2 * p + side
            gm = gp * sides[side]
            for ib, ub in tiles:
                mi, mu = slice(ib * hb, ib * hb + hb), slice(ub * hb, ub * hb + hb)
                mixed_t = lax.dot_general(xp[mi], gm[mu], NT, preferred_element_type=F32)
                decay_t = jnp.exp(jnp.minimum(row_v[h : h + 1, mu] - cols_v[h, mi, :], 0.0))
                if ib == ub:
                    decay_t = jnp.where(tri, decay_t, 0.0)
                first_t = mixed_t * decay_t
                if h == 0:
                    acc_f[mi, mu] = first_t
                else:
                    acc_f[mi, mu] += first_t
                third_t = (gram_t[mi, mu] * decay_t).astype(BF16)
                out[ib] = out[ib] + jnp.dot(third_t, gm[mu], preferred_element_type=F32)
        gx_acc[:hb, at] = out[0]
        gx_acc[hb:, at] = out[1]
    acc_f[hb:, :hb] = jnp.zeros((hb, hb), F32)
    first_t = acc_f[...]
    part[1] = jnp.dot(first_t.astype(BF16), c_v[...], preferred_element_type=F32)
    part[0] = jnp.dot(first_t.T.astype(BF16), b_v[...], preferred_element_type=F32)

    @pl.when(first)
    def _():
        pl.semaphore_wait(row_in, ny - 1)
        for z in range(1, nz):
            signal(rows_in, at_z(z))

    pl.when(me_z > 0)(lambda: pl.semaphore_wait(rows_in, 1))
    for to in y_to:
        remote(own_row, dec_y.at[me_y], dy_send, dy_recv, at_y(to)).start()

    def y_copy(way, part_at, y):
        chunk = way * HALVES + part_at
        return remote(
            total.at[way, part_at],
            rec_y.at[way, part_at, me_y],
            y_send.at[chunk, y],
            y_recv.at[chunk, me_y],
            at_y(y),
        )

    def y_from(way, part_at, y):
        chunk = way * HALVES + part_at
        return remote(
            total.at[way, part_at],
            rec_y.at[way, part_at, y],
            y_send.at[chunk, y],
            y_recv.at[chunk, y],
            at_y(y),
        )

    def y_targets(way, fn):
        for off in reversed(range(1, ny)):
            y = me_y + off if way == FORWARD else me_y - off
            pl.when((y < ny) & (y >= 0))(functools.partial(fn, y))

    def scan_row(way, part_at):
        wait_bytes(rec_z.at[way, part_at, others_z], z_recv.at[way * HALVES + part_at])
        state = jnp.zeros((half, width), F32)
        for z in range(nz) if way == FORWARD else reversed(range(nz)):
            pre[way, part_at, z] = state
            state = state * dec_z[z] + rec_z[way, part_at, z]
        total[way, part_at] = state
        y_targets(way, lambda y: y_copy(way, part_at, y).start())

    def carry_row(way, part_at):
        def body(i, state):
            y = i if way == FORWARD else ny - 1 - i
            y_from(way, part_at, y).wait_recv()
            return state * dec_y[y] + rec_y[way, part_at, y]

        steps = me_y if way == FORWARD else ny - 1 - me_y
        state = lax.fori_loop(0, steps, body, jnp.zeros((half, width), F32))
        for z in range(nz):
            back[way, part_at, z] = pre[way, part_at, z] + edge[way, z] * state
        ret[way, part_at, me_z] = back[way, part_at, me_z]

    def give_back(way, part_at, targets):
        chunk = way * HALVES + part_at
        for to in targets:
            remote(
                back.at[way, part_at, to],
                ret.at[way, part_at, me_z],
                r_send.at[chunk],
                r_recv.at[chunk],
                at_z(to),
            ).start()

    cut = (nz - 1) // 2
    early, late = z_up[:cut], z_up[cut:]
    scan_row(FORWARD, 0)
    scan_row(BACKWARD, 0)
    wait_bytes(dec_y.at[others_y], dy_recv)
    carry_row(FORWARD, 0)
    give_back(FORWARD, 0, z_up)
    scan_row(FORWARD, 1)
    carry_row(BACKWARD, 0)
    give_back(BACKWARD, 0, z_up)
    scan_row(BACKWARD, 1)
    carry_row(FORWARD, 1)
    give_back(FORWARD, 1, z_up[:2])
    carry_row(BACKWARD, 1)
    give_back(BACKWARD, 1, z_up[:2])
    give_back(FORWARD, 1, z_up[2:])
    give_back(BACKWARD, 1, z_up[2:])

    def collect(way):
        for part_at in range(HALVES):
            wait_bytes(ret.at[way, part_at, others_z], r_recv.at[way * HALVES + part_at])
        for z in range(nz):
            both = jnp.concatenate([ret[way, part_at, z] for part_at in range(HALVES)], axis=0)
            hbf[way, z * piece : z * piece + piece] = both.astype(BF16)

    def share(way):
        for to in t_to:
            remote(
                part.at[way, pl.ds(pl.multiple_of(to * rows, rows), rows)],
                rec_t.at[way, me_t],
                t_send.at[way],
                t_recv.at[way],
                at_t(to),
            ).start()
        rec_t[way, me_t] = part[way, pl.ds(pl.multiple_of(me_t * rows, rows), rows)]

    collect(FORWARD)
    part[0] += lax.dot_general(gw_v[...], hbf[FORWARD], NT, preferred_element_type=F32)
    share(0)
    collect(BACKWARD)
    part[1] += lax.dot_general(xw_v[...], hbf[BACKWARD], NT, preferred_element_type=F32)
    share(1)
    inter = jnp.dot(b_v[...], hbf[BACKWARD], preferred_element_type=F32)
    gx_out[...] = (gx_acc[...] + tail_v[...] * inter).astype(BF16)

    wait_bytes(dec_z.at[others_z], dz_send)
    wait_bytes(dec_y.at[others_y], dy_send)
    for way in (FORWARD, BACKWARD):
        for part_at in range(HALVES):
            chunk = way * HALVES + part_at
            wait_bytes(rec_z.at[way, part_at, others_z], z_send.at[chunk])
            wait_bytes(ret.at[way, part_at, others_z], r_send.at[chunk])
            y_targets(way, lambda y: y_copy(way, part_at, y).wait_send())
    for way, out in ((0, gc_out), (1, gb_out)):
        wait_bytes(rec_t.at[way, others_t], t_recv.at[way])
        out[...] = jnp.sum(rec_t[way], axis=0)
        wait_bytes(rec_t.at[way, others_t], t_send.at[way])


def write_kernel(gx, gb, gc, gx_hbm, gb_hbm, gc_hbm, sem):
    copies = [
        pltpu.make_async_copy(src, dst, sem.at[i])
        for i, (src, dst) in enumerate(((gx, gx_hbm), (gb, gb_hbm), (gc, gc_hbm)))
    ]
    for copy in copies:
        copy.start()
    for copy in copies:
        copy.wait()


def shards(x_heads, log_decay, b_proj, c_proj, grad_out):
    blocks, nt = lax.axis_size("ctx"), lax.axis_size("tp")
    ny, nz = grid_of(blocks)
    heads = log_decay.shape[0]
    width = heads * HEADDIM
    piece = STATE // nz
    half = piece // HALVES
    rows = GROUP // nt
    chunks = 2 * HALVES
    in_hbm = pl.BlockSpec(memory_space=pltpu.HBM)
    in_vmem = pl.BlockSpec(memory_space=pltpu.VMEM)
    dma = pltpu.SemaphoreType.DMA
    vmem = pltpu.VMEM
    inputs = (x_heads, log_decay, b_proj, c_proj, grad_out)
    inputs = [pltpu.with_memory_space_constraint(a, pltpu.HBM) for a in inputs]
    out_shape = (
        jax.ShapeDtypeStruct((GROUP, width), BF16),
        jax.ShapeDtypeStruct((rows, STATE), F32),
        jax.ShapeDtypeStruct((rows, STATE), F32),
    )
    results = pl.pallas_call(
        functools.partial(kernel, ny, nz, nt),
        out_shape=out_shape,
        in_specs=[in_hbm] * 5,
        out_specs=[in_vmem] * 3,
        scratch_shapes=[
            vmem((GROUP, width), BF16),
            vmem((heads, GROUP), F32),
            vmem((GROUP, STATE), BF16),
            vmem((GROUP, STATE), BF16),
            vmem((GROUP, width), BF16),
            vmem((GROUP, width), BF16),
            vmem((GROUP, width), BF16),
            vmem((GROUP, width), F32),
            vmem((heads, GROUP, 128), F32),
            vmem((heads, GROUP), F32),
            vmem((1, width), F32),
            vmem((nz, 1, width), F32),
            vmem((ny, 1, width), F32),
            vmem((1, width), F32),
            vmem((2, nz, 1, width), F32),
            vmem((2, STATE, width), F32),
            vmem((2, HALVES, nz, half, width), F32),
            vmem((2, HALVES, nz, half, width), F32),
            vmem((2, HALVES, half, width), F32),
            vmem((2, HALVES, ny, half, width), F32),
            vmem((2, HALVES, nz, half, width), F32),
            vmem((2, HALVES, nz, half, width), F32),
            vmem((2, STATE, width), BF16),
            vmem((GROUP, GROUP), F32),
            vmem((GROUP, width), F32),
            vmem((2, GROUP, STATE), F32),
            vmem((2, nt, rows, STATE), F32),
            dma((5,)),
            pltpu.SemaphoreType.REGULAR,
            pltpu.SemaphoreType.REGULAR,
            dma,
            dma,
            dma,
            dma,
            dma((chunks,)),
            dma((chunks,)),
            dma((chunks, ny)),
            dma((chunks, ny)),
            dma((chunks,)),
            dma((chunks,)),
            dma((2,)),
            dma((2,)),
        ],
        compiler_params=pltpu.CompilerParams(
            collective_id=0, has_side_effects=True, vmem_limit_bytes=48 * 1024 * 1024
        ),
        name="mixer_backward",
    )(*inputs)
    return pl.pallas_call(
        write_kernel,
        out_shape=out_shape,
        in_specs=[pl.BlockSpec(memory_space=pl.ANY)] * 3,
        out_specs=[in_hbm] * 3,
        scratch_shapes=[dma((3,))],
        compiler_params=pltpu.CompilerParams(vmem_limit_bytes=1024 * 1024),
        name="write_out",
    )(*results)


def solution(mesh):
    in_specs = (P("ctx", "tp"), P("tp", "ctx"), P("ctx", None), P("ctx", None), P("ctx", "tp"))
    out_specs = (P("ctx", "tp"), P(("ctx", "tp"), None), P(("ctx", "tp"), None))
    return jax.shard_map(shards, mesh=mesh, in_specs=in_specs, out_specs=out_specs, check_vma=False)
```
